32 devices in a mesh: dp: 8 (over z, x), tensor: 4 (over y, core).
Axes of the slice: x: 2, y: 2, z: 4, core: 2. Of those that a mesh axis runs over, the one named last changes fastest.
Arguments:
- features: bfloat16 [3072, 8192], P('dp', 'tensor'), may hold values from -6 to 6
- key_value_weight: bfloat16 [8192, 2048], P('tensor'), may hold values from -0.0625 to 0.0625
- adapter_down_weight: bfloat16 [32, 64, 8192], P('dp', None, 'tensor'), may hold values from -0.0625 to 0.0625
- adapter_up_weight: bfloat16 [32, 64, 2048], P('dp', None, 'tensor'), may hold values from -0.75 to 0.75
- token_adapter_index: int32 [3072], P('dp'), may hold values from 0 to 31, as said below
- adapter_position: int32 [32], replicated, may hold values from 0 to 31, as said below
- output_gradient: bfloat16 [3072, 2048], P('dp', 'tensor'), may hold values from -6 to 6
Outputs:
- key_value_output: bfloat16 [3072, 2048], P('dp', 'tensor')
- feature_gradient: bfloat16 [3072, 8192], P('dp', 'tensor')
- down_gradient: float32 [32, 64, 8192], P('dp', None, 'tensor')
- up_gradient: float32 [32, 64, 2048], P('dp', None, 'tensor')
The draws below stay inside these ranges and needn't reach their ends.
Inputs may be any that keep to these rules, and one draw needn't show every extreme that they name: `token_adapter_index`: within each aligned block of 384 tokens (those of one index of dp) the ids do not fall. Call slot // 4 the storing index of an adapter; in each block at most 144 tokens have adapters of one storing index. In every draw one storing index, the same for all blocks, gets exactly 144 tokens from every block, and in every block another storing index, which varies from block to block, gets exactly 144 tokens as well. A permutation: adapter a is stored at slot adapter_position[a].
All inputs are finite; a program needn't handle non-finite values.
Results may differ from the reference program's by a relative error of at most 0.0054.
Values may be sent and summed in bfloat16 or wider, within the bound.
A program may use at most 64 MiB of HBM per device.

```python
import jax
import jax.numpy as jnp
from jax import lax

MODEL_WIDTH = 8192
ADAPTER_RANK = 64
ADAPTERS_PER_DP = 4
TOK_GRP = 384
KEY_VALUE_WIDTH = 2048
ADAPTER_TOTAL = 32
TOKENS = 3072
CAP = 144
N_DP = 8


def adapter_placement(key):
    return jax.random.permutation(jax.random.fold_in(key, 7), ADAPTER_TOTAL).astype(jnp.int32)


def draw_adapter_position(key, part):
    return adapter_placement(key)


def draw_token_adapter_index(key, part):
    slots = adapter_placement(key)
    inverse = jnp.argsort(slots, stable=True).astype(jnp.int32)
    hottest = jax.random.randint(jax.random.fold_in(key, 11), (), 0, N_DP).astype(jnp.int32)
    remain = TOK_GRP - 2 * CAP
    others = jnp.arange(N_DP - 1, dtype=jnp.int32)
    others = others + (others >= hottest).astype(jnp.int32)

    def one_group(index):
        group_key = jax.random.fold_in(jax.random.fold_in(key, 13), index)
        second_owner = others[jax.random.randint(jax.random.fold_in(group_key, 3), (), 0, N_DP - 1)].astype(jnp.int32)
        lower_owner = jnp.minimum(hottest, second_owner)
        upper_owner = jnp.maximum(hottest, second_owner)
        rest_owners = jnp.arange(N_DP - 2, dtype=jnp.int32)
        rest_owners = rest_owners + (rest_owners >= lower_owner).astype(jnp.int32)
        rest_owners = rest_owners + (rest_owners >= upper_owner).astype(jnp.int32)
        weights = jax.random.randint(jax.random.fold_in(group_key, 1), (N_DP - 2,), 1, 4).astype(jnp.int32)
        bounds = jnp.cumsum(weights) * remain // jnp.sum(weights)
        places = jnp.arange(remain, dtype=jnp.int32)
        which = jnp.sum((bounds[None, :] <= places[:, None]).astype(jnp.int32), axis=1)
        owners = jnp.concatenate([jnp.zeros((CAP,), jnp.int32) + hottest, jnp.zeros((CAP,), jnp.int32) + second_owner, rest_owners[which]])
        within = jax.random.randint(jax.random.fold_in(group_key, 2), (TOK_GRP,), 0, ADAPTERS_PER_DP).astype(jnp.int32)
        chosen = inverse[owners * ADAPTERS_PER_DP + within]
        return jnp.sort(chosen)
    return jax.vmap(one_group)(jnp.arange(N_DP, dtype=jnp.int32)).reshape(TOKENS).astype(jnp.int32)


def level_of(own_key, dims, pieces, least, top_value):
    gain, own = 1.0, jax.random.fold_in(own_key, 6)
    for axis_at, parts in pieces:
        draws = jnp.exp(jax.random.uniform(jax.random.fold_in(own, axis_at), (parts,), jnp.float32, least / len(pieces), top_value / len(pieces)))
        gain = gain * jnp.repeat(draws, dims[axis_at] // parts).reshape([-1 if axis == axis_at else 1 for axis in range(len(dims))])
    return gain


def centred(own_key, extent, width, most, cuts=(), kind=jnp.bfloat16):
    factor_of = level_of(own_key, extent, cuts, -0.22, 0.18) if cuts else 1.0
    values = jax.random.normal(own_key, extent, jnp.float32) * width * factor_of
    return jnp.minimum(jnp.maximum(values, -most), most).astype(kind)


def setup_inputs(seed: int = 0) -> dict:
    keys = jax.random.split(jax.random.key(seed), 8)
    return {
        "features": centred(keys[0], (TOKENS, MODEL_WIDTH), 1.0, 6.0, ((0, 8), (1, 4))),
        "key_value_weight": centred(keys[1], (MODEL_WIDTH, KEY_VALUE_WIDTH), MODEL_WIDTH ** -0.5, 0.0625, ((0, 4),)),
        "adapter_down_weight": centred(keys[2], (ADAPTER_TOTAL, ADAPTER_RANK, MODEL_WIDTH), MODEL_WIDTH ** -0.5, 0.0625, ((0, 8), (2, 4))),
        "adapter_up_weight": centred(keys[3], (ADAPTER_TOTAL, ADAPTER_RANK, KEY_VALUE_WIDTH), ADAPTER_RANK ** -0.5, 0.75, ((0, 8), (2, 4))),
        "token_adapter_index": draw_token_adapter_index(jax.random.fold_in(keys[7], 71), 0),
        "adapter_position": draw_adapter_position(jax.random.fold_in(keys[7], 71), 0),
        "output_gradient": centred(keys[6], (TOKENS, KEY_VALUE_WIDTH), 1.0, 6.0, ((0, 8), (1, 4))),
    }


adapter_scale = 2.0


def reference(features, key_value_weight, adapter_down_weight, adapter_up_weight, token_adapter_index, adapter_position, output_gradient):
    highest_precision = lax.Precision.HIGHEST
    weight_wide = key_value_weight.astype(jnp.float32)
    key_value_frozen = jnp.dot(features.astype(jnp.float32), weight_wide, precision=highest_precision)
    gradient_frozen = jnp.dot(output_gradient.astype(jnp.float32), weight_wide.T, precision=highest_precision)
    slot_tok = adapter_position[token_adapter_index].astype(jnp.int32)
    owner_of = slot_tok // ADAPTERS_PER_DP
    local_id = slot_tok % ADAPTERS_PER_DP
    lane_ids = jnp.arange(ADAPTERS_PER_DP * ADAPTER_RANK, dtype=jnp.int32) // ADAPTER_RANK
    holding_rows = N_DP * CAP

    def rows_per_holder(loop_carry, owner):
        adapter_full_output, input_adapter_rows = loop_carry
        found_match = jnp.nonzero(owner_of == owner, size=holding_rows, fill_value=TOKENS)[0].astype(jnp.int32)
        valid = (found_match < TOKENS).astype(jnp.float32)
        safe = jnp.minimum(found_match, TOKENS - 1)
        rows_in = features[safe].astype(jnp.float32) * valid[:, None]
        incoming_gradients = output_gradient[safe].astype(jnp.float32) * valid[:, None]
        slot_selector = (lane_ids[None, :] == local_id[safe][:, None]).astype(jnp.float32) * valid[:, None]
        offset_start = (owner * ADAPTERS_PER_DP).astype(jnp.int32)
        down_matrix = lax.dynamic_slice_in_dim(adapter_down_weight, offset_start, ADAPTERS_PER_DP, 0).reshape(ADAPTERS_PER_DP * ADAPTER_RANK, MODEL_WIDTH).astype(jnp.float32)
        up_matrix = lax.dynamic_slice_in_dim(adapter_up_weight, offset_start, ADAPTERS_PER_DP, 0).reshape(ADAPTERS_PER_DP * ADAPTER_RANK, KEY_VALUE_WIDTH).astype(jnp.float32)
        down_total = jnp.sum((jnp.dot(rows_in, down_matrix.T, precision=highest_precision) * slot_selector).reshape(holding_rows, ADAPTERS_PER_DP, ADAPTER_RANK), axis=1)
        down_round = lax.optimization_barrier(down_total.astype(jnp.bfloat16)).astype(jnp.float32)
        down_gathered = jnp.tile(down_round, (1, ADAPTERS_PER_DP)) * slot_selector
        adapter_row_block = (adapter_scale * jnp.dot(down_gathered, up_matrix, precision=highest_precision)).astype(jnp.bfloat16)
        up_combined = jnp.sum((adapter_scale * jnp.dot(incoming_gradients, up_matrix.T, precision=highest_precision) * slot_selector).reshape(holding_rows, ADAPTERS_PER_DP, ADAPTER_RANK), axis=1)
        up_round = lax.optimization_barrier(up_combined.astype(jnp.bfloat16)).astype(jnp.float32)
        up_wide = jnp.tile(up_round, (1, ADAPTERS_PER_DP)) * slot_selector
        input_row_block = jnp.dot(up_wide, down_matrix, precision=highest_precision).astype(jnp.bfloat16)
        down_gradient = jnp.dot(up_wide.T, rows_in, precision=highest_precision).reshape(ADAPTERS_PER_DP, ADAPTER_RANK, MODEL_WIDTH)
        up_gradient = (adapter_scale * jnp.dot(down_gathered.T, incoming_gradients, precision=highest_precision)).reshape(ADAPTERS_PER_DP, ADAPTER_RANK, KEY_VALUE_WIDTH)
        adapter_full_output = adapter_full_output.at[found_match].add(adapter_row_block.astype(jnp.float32), mode="drop")
        input_adapter_rows = input_adapter_rows.at[found_match].add(input_row_block.astype(jnp.float32), mode="drop")
        return (adapter_full_output, input_adapter_rows), (down_gradient, up_gradient)

    initial_carry = (jnp.zeros((TOKENS, KEY_VALUE_WIDTH), jnp.float32), jnp.zeros((TOKENS, MODEL_WIDTH), jnp.float32))
    (adapter_full_output, input_adapter_rows), (down_gradient_list, up_gradient_list) = lax.scan(rows_per_holder, initial_carry, jnp.arange(N_DP, dtype=jnp.int32))
    key_value_output = (key_value_frozen + adapter_full_output).astype(jnp.bfloat16)
    feature_gradient = (gradient_frozen + input_adapter_rows).astype(jnp.bfloat16)
    return key_value_output, feature_gradient, down_gradient_list.reshape(ADAPTER_TOTAL, ADAPTER_RANK, MODEL_WIDTH), up_gradient_list.reshape(ADAPTER_TOTAL, ADAPTER_RANK, KEY_VALUE_WIDTH)
```

```python
import functools

import jax
import jax.numpy as jnp
from jax import lax
from jax.experimental import pallas as pl
from jax.experimental.pallas import tpu as pltpu
from jax.sharding import PartitionSpec as P

adapter_scale = 2.0


def dot_dims(left, right, left_dim, right_dim):
    return lax.dot_general(
        left, right, (((left_dim,), (right_dim,)), ((), ())), preferred_element_type=jnp.float32
    )


def slot_mask(slot_row, rank, rows):
    tokens = slot_row.shape[1]
    row_slot = lax.broadcasted_iota(jnp.int32, (rows, tokens), 0) // rank
    return row_slot == slot_row


def project_kernel(rank, scale, slot_ref, x_ref, w_ref, o_ref):
    rows = w_ref.shape[0]
    full = dot_dims(w_ref[...], x_ref[...], 1, 1)
    kept = jnp.where(slot_mask(slot_ref[...], rank, rows), full, 0.0)
    o_ref[0] = scale * jnp.sum(kept.reshape(rows // rank, rank, kept.shape[1]), axis=0)


def widen(values, slot_row, rows):
    rank = values.shape[0]
    tiled = jnp.tile(values.astype(jnp.float32), (rows // rank, 1))
    return jnp.where(slot_mask(slot_row, rank, rows), tiled, 0.0).astype(jnp.bfloat16)


def back_kernel(slot_ref, up_ref, x_ref, w_ref, rows_ref, grad_ref, total):
    step = pl.program_id(0)
    wide = widen(up_ref[0], slot_ref[...], w_ref.shape[0])
    rows_ref[...] = dot_dims(wide, w_ref[...], 0, 0).astype(rows_ref.dtype)
    part = jnp.dot(wide, x_ref[...], preferred_element_type=jnp.float32)

    @pl.when(step == 0)
    def _():
        total[...] = part

    @pl.when(step > 0)
    def _():
        total[...] += part

    @pl.when(step == pl.num_programs(0) - 1)
    def _():
        grad_ref[...] = total[...].astype(grad_ref.dtype)


def up_grad_kernel(slot_ref, down_ref, dy_ref, grad_ref, total):
    step = pl.program_id(0)
    wide = widen(down_ref[0], slot_ref[...], grad_ref.shape[1])
    part = dot_dims(dy_ref[...], wide, 1, 1)

    @pl.when(step == 0)
    def _():
        total[...] = part

    @pl.when(step > 0)
    def _():
        total[...] += part

    @pl.when(step == pl.num_programs(0) - 1)
    def _():
        grad_ref[...] = (adapter_scale * total[...]).astype(grad_ref.dtype)


def out_kernel(slot_ref, down_ref, w_ref, base_ref, o_ref):
    wide = widen(down_ref[...], slot_ref[...], w_ref.shape[0])
    rows = (adapter_scale * dot_dims(wide, w_ref[...], 0, 0)).astype(jnp.bfloat16)
    o_ref[...] = (base_ref[...] + rows.astype(jnp.float32)).astype(o_ref.dtype)


def cost(flops, nbytes):
    return pl.CostEstimate(flops=int(flops), bytes_accessed=int(nbytes), transcendentals=0)


def project(slots, x, w, rank, tokens, scale, name):
    total_tokens, width = x.shape
    rows = w.shape[0]
    blocks = total_tokens // tokens
    return pl.pallas_call(
        functools.partial(project_kernel, rank, scale),
        out_shape=jax.ShapeDtypeStruct((blocks, rank, tokens), jnp.float32),
        grid=(blocks,),
        in_specs=[
            pl.BlockSpec((1, tokens), lambda i: (0, i)),
            pl.BlockSpec((tokens, width), lambda i: (i, 0)),
            pl.BlockSpec((rows, width), lambda i: (0, 0)),
        ],
        out_specs=pl.BlockSpec((1, rank, tokens), lambda i: (i, 0, 0)),
        cost_estimate=cost(2 * total_tokens * rows * width, 2 * (total_tokens + rows) * width),
        name=name,
    )(slots, x, w)


def back(slots, up_all, x, w, tokens):
    total_tokens, width = x.shape
    rows = w.shape[0]
    rank = up_all.shape[1]
    blocks = total_tokens // tokens
    return pl.pallas_call(
        back_kernel,
        out_shape=(
            jax.ShapeDtypeStruct((total_tokens, width), jnp.bfloat16),
            jax.ShapeDtypeStruct((rows, width), jnp.bfloat16),
        ),
        grid=(blocks,),
        in_specs=[
            pl.BlockSpec((1, tokens), lambda i: (0, i)),
            pl.BlockSpec((1, rank, tokens), lambda i: (i, 0, 0)),
            pl.BlockSpec((tokens, width), lambda i: (i, 0)),
            pl.BlockSpec((rows, width), lambda i: (0, 0)),
        ],
        out_specs=(
            pl.BlockSpec((tokens, width), lambda i: (i, 0)),
            pl.BlockSpec((rows, width), lambda i: (0, 0)),
        ),
        scratch_shapes=[pltpu.VMEM((rows, width), jnp.float32)],
        cost_estimate=cost(4 * total_tokens * rows * width, 4 * (total_tokens + rows) * width),
        name="back",
    )(slots, up_all, x, w)


def up_grad(slots, down_all, dy, rows, tokens):
    width, total_tokens = dy.shape
    rank = down_all.shape[1]
    blocks = total_tokens // tokens
    return pl.pallas_call(
        up_grad_kernel,
        out_shape=jax.ShapeDtypeStruct((width, rows), jnp.bfloat16),
        grid=(blocks,),
        in_specs=[
            pl.BlockSpec((1, tokens), lambda i: (0, i)),
            pl.BlockSpec((1, rank, tokens), lambda i: (i, 0, 0)),
            pl.BlockSpec((width, tokens), lambda i: (0, i)),
        ],
        out_specs=pl.BlockSpec((width, rows), lambda i: (0, 0)),
        scratch_shapes=[pltpu.VMEM((width, rows), jnp.float32)],
        cost_estimate=cost(2 * total_tokens * rows * width, 2 * (total_tokens + rows) * width),
        name="up_grad",
    )(slots, down_all, dy)


def add_out(slots, down, w, base):
    tokens, width = base.shape
    return pl.pallas_call(
        out_kernel,
        out_shape=jax.ShapeDtypeStruct((tokens, width), jnp.bfloat16),
        cost_estimate=cost(2 * tokens * w.shape[0] * width, 2 * w.shape[0] * width),
        name="add_out",
    )(slots, down, w, base)


def body(
    features,
    key_value_weight,
    adapter_down_weight,
    adapter_up_weight,
    token_adapter_index,
    adapter_position,
    output_gradient,
):
    tokens, width_local = features.shape
    output_local = output_gradient.shape[1]
    local_count, rank, _ = adapter_down_weight.shape
    all_count = adapter_position.shape[0]
    down_matrix = adapter_down_weight.reshape(local_count * rank, width_local)
    up_matrix = adapter_up_weight.reshape(local_count * rank, output_local)

    def exchange(array, split, concat):
        return lax.all_to_all(array, "dp", split_axis=split, concat_axis=concat, tiled=True)

    up_rows = lax.all_gather(up_matrix, "dp", axis=0, tiled=True)
    ids = jnp.arange(all_count, dtype=jnp.int32)
    matches = token_adapter_index[:, None] == ids[None, :]
    slot_tok = jnp.sum(jnp.where(matches, adapter_position[None, :], 0), axis=1)
    slots = slot_tok.reshape(1, tokens)
    slots_all = lax.all_gather(slot_tok, "dp", axis=0, tiled=True).reshape(1, -1)

    down_cols = exchange(down_matrix, 1, 0)
    feature_cols = exchange(features, 1, 0)
    dy_cols = exchange(output_gradient.T, 0, 1)

    up_part = project(slots, output_gradient, up_rows, rank, tokens, adapter_scale, "up_back")
    up_own = lax.psum(up_part[0], "tensor").astype(jnp.bfloat16)
    up_all = lax.all_gather(up_own, "dp", axis=0, tiled=False)

    down_part = project(slots_all, feature_cols, down_cols, rank, tokens, 1.0, "down")
    down_all = lax.psum(down_part, ("dp", "tensor")).astype(jnp.bfloat16)

    in_cols, down_grad_cols = back(slots_all, up_all, feature_cols, down_cols, tokens)
    lora_in = exchange(in_cols, 0, 1)
    down_gradient = exchange(down_grad_cols, 0, 1)

    up_grad_cols = up_grad(slots_all, down_all, dy_cols, all_count * rank, tokens)
    up_gradient = exchange(up_grad_cols, 1, 0)

    gradient_frozen = dot_dims(
        lax.all_gather(output_gradient, "tensor", axis=1, tiled=True), key_value_weight, 1, 1
    )
    key_value_frozen = lax.psum_scatter(
        dot_dims(key_value_weight, features, 0, 1), "tensor", scatter_dimension=0, tiled=True
    ).T
    down_own = lax.dynamic_index_in_dim(down_all, lax.axis_index("dp"), 0, keepdims=False)
    key_value_output = add_out(slots, down_own, up_rows, key_value_frozen)
    feature_gradient = (gradient_frozen + lora_in.astype(jnp.float32)).astype(jnp.bfloat16)
    return (
        key_value_output,
        feature_gradient,
        down_gradient.astype(jnp.float32).reshape(local_count, rank, width_local),
        up_gradient.astype(jnp.float32).T.reshape(local_count, rank, output_local),
    )


def solution(mesh):
    placed = (
        P("dp", "tensor"),
        P("tensor", None),
        P("dp", None, "tensor"),
        P("dp", None, "tensor"),
        P("dp"),
        P(),
        P("dp", "tensor"),
    )
    return jax.shard_map(
        body,
        mesh=mesh,
        in_specs=placed,
        out_specs=(
            P("dp", "tensor"),
            P("dp", "tensor"),
            P("dp", None, "tensor"),
            P("dp", None, "tensor"),
        ),
        check_vma=False,
    )
```

```python
import functools

import jax
import jax.numpy as jnp
from jax import lax
from jax.experimental import pallas as pl
from jax.experimental.pallas import tpu as pltpu
from jax.sharding import PartitionSpec as P

adapter_scale = 2.0


def dot_dims(left, right, left_dim, right_dim):
    return lax.dot_general(
        left, right, (((left_dim,), (right_dim,)), ((), ())), preferred_element_type=jnp.float32
    )


def slot_mask(slot_row, rank, rows):
    tokens = slot_row.shape[1]
    row_slot = lax.broadcasted_iota(jnp.int32, (rows, tokens), 0) // rank
    return row_slot == slot_row


def fold_slots(full, slot_row, rank):
    rows, tokens = full.shape
    kept = jnp.where(slot_mask(slot_row, rank, rows), full, 0.0)
    return jnp.sum(kept.reshape(rows // rank, rank, tokens), axis=0)


def down_kernel(rank, slot_ref, x_ref, w_ref, o_ref):
    full = dot_dims(w_ref[...], x_ref[...], 1, 1)
    o_ref[0] = fold_slots(full, slot_ref[...], rank).astype(o_ref.dtype)


def up_kernel(rank, slot_ref, dy_ref, w_ref, o_ref):
    full = dot_dims(w_ref[...], dy_ref[0, : w_ref.shape[0]], 0, 0)
    o_ref[0] = (adapter_scale * fold_slots(full, slot_ref[...], rank)).astype(o_ref.dtype)


def widen(values, slot_row, rows):
    rank = values.shape[0]
    tiled = jnp.tile(values.astype(jnp.float32), (rows // rank, 1))
    return jnp.where(slot_mask(slot_row, rank, rows), tiled, 0.0).astype(jnp.bfloat16)


def back_kernel(slot_ref, up_ref, x_ref, w_ref, rows_ref, grad_ref, total):
    step = pl.program_id(0)
    wide = widen(up_ref[0], slot_ref[...], w_ref.shape[0])
    rows_ref[...] = dot_dims(wide, w_ref[...], 0, 0).astype(rows_ref.dtype)
    part = jnp.dot(wide, x_ref[...], preferred_element_type=jnp.float32)

    @pl.when(step == 0)
    def _():
        total[...] = part

    @pl.when(step > 0)
    def _():
        total[...] += part

    @pl.when(step == pl.num_programs(0) - 1)
    def _():
        grad_ref[...] = total[...].astype(grad_ref.dtype)


def up_grad_kernel(slot_ref, down_ref, dy_ref, w_ref, rows_ref, grad_ref, total):
    step = pl.program_id(0)
    width, rows = w_ref.shape
    wide = widen(down_ref[0], slot_ref[...], rows)
    out = jnp.dot(w_ref[...], wide, preferred_element_type=jnp.float32)
    rows_ref[0] = (adapter_scale * out).astype(rows_ref.dtype)
    part = dot_dims(dy_ref[0, :width], wide, 1, 1)

    @pl.when(step == 0)
    def _():
        total[...] = part

    @pl.when(step > 0)
    def _():
        total[...] += part

    @pl.when(step == pl.num_programs(0) - 1)
    def _():
        grad_ref[...] = (adapter_scale * total[...]).astype(grad_ref.dtype)


def sum_kernel(n_d, n_t, part_ref, out_ref, from_t, own_t, from_d, own_d, all_d, send, recv):
    me_d, me_t = lax.axis_index("dp"), lax.axis_index("tensor")
    peers_d = [lax.rem(me_d + k, n_d) for k in range(n_d)]
    peers_t = [lax.rem(me_t + k, n_t) for k in range(n_t)]

    barrier = pltpu.get_barrier_semaphore()
    for peer in peers_t[1:]:
        pl.semaphore_signal(
            barrier, inc=1, device_id=(me_d, peer), device_id_type=pl.DeviceIdType.MESH
        )
    for peer in peers_d[1:]:
        pl.semaphore_signal(
            barrier, inc=1, device_id=(peer, me_t), device_id_type=pl.DeviceIdType.MESH
        )
    pl.semaphore_wait(barrier, n_d + n_t - 2)

    base = 0

    def copy(src, dst, device, index):
        made = pltpu.make_async_remote_copy(
            src_ref=src,
            dst_ref=dst,
            send_sem=send.at[index],
            recv_sem=recv.at[index],
            device_id=device,
            device_id_type=pl.DeviceIdType.MESH,
        )
        made.start()
        return made

    made = [
        copy(part_ref.at[:, peers_t[k]], from_t.at[k - 1], (me_d, peers_t[k]), base + k - 1)
        for k in range(1, n_t)
    ]
    base += n_t - 1
    for one in made:
        one.wait()
    total = part_ref[:, me_t].astype(jnp.float32)
    for k in range(n_t - 1):
        total = total + from_t[k].astype(jnp.float32)
    own_t[...] = total.astype(own_t.dtype)

    made = [
        copy(own_t.at[peers_d[k]], from_d.at[k - 1], (peers_d[k], me_t), base + k - 1)
        for k in range(1, n_d)
    ]
    base += n_d - 1
    for one in made:
        one.wait()
    total = own_t[me_d].astype(jnp.float32)
    for k in range(n_d - 1):
        total = total + from_d[k].astype(jnp.float32)
    own_d[...] = total.astype(own_d.dtype)

    made = [
        copy(own_d, all_d.at[me_d], (peers_d[k], me_t), base + k - 1) for k in range(1, n_d)
    ]
    base += n_d - 1
    all_d[me_d] = own_d[...]
    for one in made:
        one.wait()

    made = [
        copy(all_d, out_ref.at[:, me_t], (me_d, peers_t[k]), base + k - 1)
        for k in range(1, n_t)
    ]
    out_ref[:, me_t] = all_d[...]
    for one in made:
        one.wait()


def cost(flops, nbytes):
    return pl.CostEstimate(flops=int(flops), bytes_accessed=int(nbytes), transcendentals=0)


def sum_all(part):
    n_d, n_t = lax.axis_size("dp"), lax.axis_size("tensor")
    _, rank, tokens = part.shape
    q = rank // n_t
    vmem = pl.BlockSpec(memory_space=pltpu.VMEM)
    copies = 2 * (n_d + n_t - 2)
    return pl.pallas_call(
        functools.partial(sum_kernel, n_d, n_t),
        out_shape=jax.ShapeDtypeStruct((n_d, n_t, q, tokens), part.dtype),
        in_specs=[vmem],
        out_specs=vmem,
        scratch_shapes=[
            pltpu.VMEM((n_t - 1, n_d, q, tokens), part.dtype),
            pltpu.VMEM((n_d, q, tokens), part.dtype),
            pltpu.VMEM((n_d - 1, q, tokens), part.dtype),
            pltpu.VMEM((q, tokens), part.dtype),
            pltpu.VMEM((n_d, q, tokens), part.dtype),
            pltpu.SemaphoreType.DMA((copies,)),
            pltpu.SemaphoreType.DMA((copies,)),
        ],
        compiler_params=pltpu.CompilerParams(collective_id=0, has_side_effects=True),
        cost_estimate=cost(1e9, 4e7),
        name="sum_all",
    )(part.reshape(n_d, n_t, q, tokens)).reshape(n_d, rank, tokens)


def project_down(slots, x, w, rank, tokens):
    total_tokens, width = x.shape
    rows = w.shape[0]
    blocks = total_tokens // tokens
    return pl.pallas_call(
        functools.partial(down_kernel, rank),
        out_shape=jax.ShapeDtypeStruct((blocks, rank, tokens), jnp.bfloat16),
        grid=(blocks,),
        in_specs=[
            pl.BlockSpec((1, tokens), lambda i: (0, i)),
            pl.BlockSpec((tokens, width), lambda i: (i, 0)),
            pl.BlockSpec((rows, width), lambda i: (0, 0)),
        ],
        out_specs=pl.BlockSpec((1, rank, tokens), lambda i: (i, 0, 0)),
        cost_estimate=cost(2 * total_tokens * rows * width, 2 * (total_tokens + rows) * width),
        name="down",
    )(slots, x, w)


def project_up(slots, dy, w, rank):
    blocks, dy_rows, tokens = dy.shape
    width, rows = w.shape
    return pl.pallas_call(
        functools.partial(up_kernel, rank),
        out_shape=jax.ShapeDtypeStruct((blocks, rank, tokens), jnp.bfloat16),
        grid=(blocks,),
        in_specs=[
            pl.BlockSpec((1, tokens), lambda i: (0, i)),
            pl.BlockSpec((1, dy_rows, tokens), lambda i: (i, 0, 0)),
            pl.BlockSpec((width, rows), lambda i: (0, 0)),
        ],
        out_specs=pl.BlockSpec((1, rank, tokens), lambda i: (i, 0, 0)),
        cost_estimate=cost(2 * blocks * tokens * rows * width, 4 * (blocks * tokens + rows) * width),
        name="up_back",
    )(slots, dy, w)


def back(slots, up_all, x, w, tokens):
    total_tokens, width = x.shape
    rows = w.shape[0]
    rank = up_all.shape[1]
    blocks = total_tokens // tokens
    return pl.pallas_call(
        back_kernel,
        out_shape=(
            jax.ShapeDtypeStruct((total_tokens, width), jnp.bfloat16),
            jax.ShapeDtypeStruct((rows, width), jnp.bfloat16),
        ),
        grid=(blocks,),
        in_specs=[
            pl.BlockSpec((1, tokens), lambda i: (0, i)),
            pl.BlockSpec((1, rank, tokens), lambda i: (i, 0, 0)),
            pl.BlockSpec((tokens, width), lambda i: (i, 0)),
            pl.BlockSpec((rows, width), lambda i: (0, 0)),
        ],
        out_specs=(
            pl.BlockSpec((tokens, width), lambda i: (i, 0)),
            pl.BlockSpec((rows, width), lambda i: (0, 0)),
        ),
        scratch_shapes=[pltpu.VMEM((rows, width), jnp.float32)],
        cost_estimate=cost(4 * total_tokens * rows * width, 4 * (total_tokens + rows) * width),
        name="back",
    )(slots, up_all, x, w)


def up_grad(slots, down_all, dy, w):
    blocks, dy_rows, tokens = dy.shape
    width, rows = w.shape
    rank = down_all.shape[1]
    return pl.pallas_call(
        up_grad_kernel,
        out_shape=(
            jax.ShapeDtypeStruct((blocks, width, tokens), jnp.bfloat16),
            jax.ShapeDtypeStruct((width, rows), jnp.bfloat16),
        ),
        grid=(blocks,),
        in_specs=[
            pl.BlockSpec((1, tokens), lambda i: (0, i)),
            pl.BlockSpec((1, rank, tokens), lambda i: (i, 0, 0)),
            pl.BlockSpec((1, dy_rows, tokens), lambda i: (i, 0, 0)),
            pl.BlockSpec((width, rows), lambda i: (0, 0)),
        ],
        out_specs=(
            pl.BlockSpec((1, width, tokens), lambda i: (i, 0, 0)),
            pl.BlockSpec((width, rows), lambda i: (0, 0)),
        ),
        scratch_shapes=[pltpu.VMEM((width, rows), jnp.float32)],
        cost_estimate=cost(4 * blocks * tokens * rows * width, 4 * (blocks * tokens + rows) * width),
        name="up_grad",
    )(slots, down_all, dy, w)


def body(
    features,
    key_value_weight,
    adapter_down_weight,
    adapter_up_weight,
    token_adapter_index,
    adapter_position,
    output_gradient,
):
    tokens, width_local = features.shape
    output_local = output_gradient.shape[1]
    local_count, rank, _ = adapter_down_weight.shape
    all_count = adapter_position.shape[0]
    down_matrix = adapter_down_weight.reshape(local_count * rank, width_local)
    up_matrix = adapter_up_weight.reshape(local_count * rank, output_local)

    groups = lax.axis_size("dp")
    part_width = output_local // groups

    def exchange(array, split, concat):
        return lax.all_to_all(array, "dp", split_axis=split, concat_axis=concat, tiled=True)

    ids = jnp.arange(all_count, dtype=jnp.int32)
    matches = token_adapter_index[:, None] == ids[None, :]
    slot_tok = jnp.sum(jnp.where(matches, adapter_position[None, :], 0), axis=1)
    digits = jnp.stack([slot_tok // 64, slot_tok % 64]).astype(jnp.bfloat16)
    pad_rows = (-part_width - 2) % 16
    tail = jnp.concatenate([digits, jnp.zeros((pad_rows, tokens), jnp.bfloat16)], axis=0)
    dy_send = jnp.concatenate(
        [
            output_gradient.T.reshape(groups, part_width, tokens),
            jnp.broadcast_to(tail[None], (groups, 2 + pad_rows, tokens)),
        ],
        axis=1,
    )
    dy_cols = exchange(dy_send, 0, 0)
    up_cols = exchange(up_matrix.T, 0, 1)
    got = dy_cols[:, part_width : part_width + 2].astype(jnp.int32)
    slots_all = (got[:, 0] * 64 + got[:, 1]).reshape(1, groups * tokens)

    down_cols = exchange(down_matrix, 1, 0)
    feature_cols = exchange(features, 1, 0)

    up_all = sum_all(project_up(slots_all, dy_cols, up_cols, rank))
    in_cols, down_grad_cols = back(slots_all, up_all, feature_cols, down_cols, tokens)
    lora_in = exchange(in_cols, 0, 1)
    down_gradient = exchange(down_grad_cols, 0, 1)

    down_all = sum_all(project_down(slots_all, feature_cols, down_cols, rank, tokens))
    out_cols, up_grad_cols = up_grad(slots_all, down_all, dy_cols, up_cols)
    lora_out = exchange(out_cols, 0, 0).reshape(output_local, tokens)
    up_gradient = exchange(up_grad_cols, 1, 0)

    gradient_frozen = dot_dims(
        lax.all_gather(output_gradient, "tensor", axis=1, tiled=True), key_value_weight, 1, 1
    )
    key_value_frozen = lax.psum_scatter(
        dot_dims(key_value_weight, features, 0, 1), "tensor", scatter_dimension=0, tiled=True
    )
    key_value_output = (key_value_frozen + lora_out.astype(jnp.float32)).astype(jnp.bfloat16).T
    feature_gradient = (gradient_frozen + lora_in.astype(jnp.float32)).astype(jnp.bfloat16)
    return (
        key_value_output,
        feature_gradient,
        down_gradient.astype(jnp.float32).reshape(local_count, rank, width_local),
        up_gradient.astype(jnp.float32).T.reshape(local_count, rank, output_local),
    )


def solution(mesh):
    placed = (
        P("dp", "tensor"),
        P("tensor", None),
        P("dp", None, "tensor"),
        P("dp", None, "tensor"),
        P("dp"),
        P(),
        P("dp", "tensor"),
    )
    return jax.shard_map(
        body,
        mesh=mesh,
        in_specs=placed,
        out_specs=(
            P("dp", "tensor"),
            P("dp", "tensor"),
            P("dp", None, "tensor"),
            P("dp", None, "tensor"),
        ),
        check_vma=False,
    )
```

```python
import functools

import jax
import jax.numpy as jnp
from jax import lax
from jax.experimental import pallas as pl
from jax.experimental.pallas import tpu as pltpu
from jax.sharding import PartitionSpec as P

adapter_scale = 2.0


def dot_dims(left, right, left_dim, right_dim):
    return lax.dot_general(
        left, right, (((left_dim,), (right_dim,)), ((), ())), preferred_element_type=jnp.float32
    )


def slot_mask(slot_row, rank, rows):
    tokens = slot_row.shape[1]
    row_slot = lax.broadcasted_iota(jnp.int32, (rows, tokens), 0) // rank
    return row_slot == slot_row


def fold_slots(full, slot_row, rank):
    rows, tokens = full.shape
    kept = jnp.where(slot_mask(slot_row, rank, rows), full, 0.0)
    return jnp.sum(kept.reshape(rows // rank, rank, tokens), axis=0)


def down_kernel(rank, slot_ref, x_ref, w_ref, o_ref):
    full = dot_dims(w_ref[...], x_ref[...], 1, 1)
    o_ref[0] = fold_slots(full, slot_ref[...], rank).astype(o_ref.dtype)


def up_kernel(rank, slot_ref, dy_ref, w_ref, o_ref):
    full = dot_dims(w_ref[...], dy_ref[0, : w_ref.shape[0]], 0, 0)
    o_ref[0] = (adapter_scale * fold_slots(full, slot_ref[...], rank)).astype(o_ref.dtype)


def widen(values, slot_row, rows):
    rank = values.shape[0]
    tiled = jnp.tile(values.astype(jnp.float32), (rows // rank, 1))
    return jnp.where(slot_mask(slot_row, rank, rows), tiled, 0.0).astype(jnp.bfloat16)


def back_kernel(slot_ref, up_ref, x_ref, w_ref, rows_ref, grad_ref, total):
    step = pl.program_id(0)
    wide = widen(up_ref[0], slot_ref[...], w_ref.shape[0])
    rows_ref[...] = dot_dims(wide, w_ref[...], 0, 0).astype(rows_ref.dtype)
    part = jnp.dot(wide, x_ref[...], preferred_element_type=jnp.float32)

    @pl.when(step == 0)
    def _():
        total[...] = part

    @pl.when(step > 0)
    def _():
        total[...] += part

    @pl.when(step == pl.num_programs(0) - 1)
    def _():
        grad_ref[...] = total[...].astype(grad_ref.dtype)


def up_grad_kernel(slot_ref, down_ref, dy_ref, w_ref, rows_ref, grad_ref, total):
    step = pl.program_id(0)
    width, rows = w_ref.shape
    wide = widen(down_ref[0], slot_ref[...], rows)
    out = jnp.dot(w_ref[...], wide, preferred_element_type=jnp.float32)
    rows_ref[0] = (adapter_scale * out).astype(rows_ref.dtype)
    part = dot_dims(dy_ref[0, :width], wide, 1, 1)

    @pl.when(step == 0)
    def _():
        total[...] = part

    @pl.when(step > 0)
    def _():
        total[...] += part

    @pl.when(step == pl.num_programs(0) - 1)
    def _():
        grad_ref[...] = (adapter_scale * total[...]).astype(grad_ref.dtype)


def sum_kernel(n_d, n_t, part_ref, out_ref, from_t, own_t, from_d, own_d, all_d, send, recv):
    me_d, me_t = lax.axis_index("dp"), lax.axis_index("tensor")
    peers_d = [lax.rem(me_d + k, n_d) for k in range(n_d)]
    peers_t = [lax.rem(me_t + k, n_t) for k in range(n_t)]

    barrier = pltpu.get_barrier_semaphore()
    for peer in peers_t[1:]:
        pl.semaphore_signal(
            barrier, inc=1, device_id=(me_d, peer), device_id_type=pl.DeviceIdType.MESH
        )
    for peer in peers_d[1:]:
        pl.semaphore_signal(
            barrier, inc=1, device_id=(peer, me_t), device_id_type=pl.DeviceIdType.MESH
        )
    pl.semaphore_wait(barrier, n_d + n_t - 2)

    base = 0

    def copy(src, dst, device, index):
        made = pltpu.make_async_remote_copy(
            src_ref=src,
            dst_ref=dst,
            send_sem=send.at[index],
            recv_sem=recv.at[index],
            device_id=device,
            device_id_type=pl.DeviceIdType.MESH,
        )
        made.start()
        return made

    made = [
        copy(part_ref.at[:, peers_t[k]], from_t.at[k - 1], (me_d, peers_t[k]), base + k - 1)
        for k in range(1, n_t)
    ]
    base += n_t - 1
    for one in made:
        one.wait()
    total = part_ref[:, me_t].astype(jnp.float32)
    for k in range(n_t - 1):
        total = total + from_t[k].astype(jnp.float32)
    own_t[...] = total.astype(own_t.dtype)

    made = [
        copy(own_t.at[peers_d[k]], from_d.at[k - 1], (peers_d[k], me_t), base + k - 1)
        for k in range(1, n_d)
    ]
    base += n_d - 1
    for one in made:
        one.wait()
    total = own_t[me_d].astype(jnp.float32)
    for k in range(n_d - 1):
        total = total + from_d[k].astype(jnp.float32)
    own_d[...] = total.astype(own_d.dtype)

    made = [
        copy(own_d, all_d.at[me_d], (peers_d[k], me_t), base + k - 1) for k in range(1, n_d)
    ]
    base += n_d - 1
    all_d[me_d] = own_d[...]
    for one in made:
        one.wait()

    made = [
        copy(all_d, out_ref.at[:, me_t], (me_d, peers_t[k]), base + k - 1)
        for k in range(1, n_t)
    ]
    out_ref[:, me_t] = all_d[...]
    for one in made:
        one.wait()


def block_view(ref, form, index, n):
    if form == "lead":
        return ref.at[index]
    width = ref.shape[1] // n
    return ref.at[:, pl.ds(pl.multiple_of(index * width, width), width)]


def exchange_kernel(n, forms, *refs):
    count = len(forms)
    sources, targets = refs[:count], refs[count : 2 * count]
    send, recv, own = refs[2 * count :]
    me_d, me_t = lax.axis_index("dp"), lax.axis_index("tensor")
    peers = [lax.rem(me_d + k, n) for k in range(n)]
    barrier = pltpu.get_barrier_semaphore()
    for peer in peers[1:]:
        pl.semaphore_signal(
            barrier, inc=1, device_id=(peer, me_t), device_id_type=pl.DeviceIdType.MESH
        )
    pl.semaphore_wait(barrier, n - 1)
    made = []
    for at, (source_form, target_form) in enumerate(forms):
        for k in range(1, n):
            made.append(
                pltpu.make_async_remote_copy(
                    src_ref=block_view(sources[at], source_form, peers[k], n),
                    dst_ref=block_view(targets[at], target_form, me_d, n),
                    send_sem=send.at[at * (n - 1) + k - 1],
                    recv_sem=recv.at[at * (n - 1) + k - 1],
                    device_id=(peers[k], me_t),
                    device_id_type=pl.DeviceIdType.MESH,
                )
            )
            made[-1].start()
    for at, (source_form, target_form) in enumerate(forms):
        made.append(
            pltpu.make_async_copy(
                block_view(sources[at], source_form, me_d, n),
                block_view(targets[at], target_form, me_d, n),
                own.at[at],
            )
        )
        made[-1].start()
    for one in made:
        one.wait()


def exchange_all(arrays, shapes, forms, collective_id):
    n = lax.axis_size("dp")
    vmem = pl.BlockSpec(memory_space=pltpu.VMEM)
    count = len(arrays)
    return pl.pallas_call(
        functools.partial(exchange_kernel, n, forms),
        out_shape=tuple(jax.ShapeDtypeStruct(shape, jnp.bfloat16) for shape in shapes),
        in_specs=[vmem] * count,
        out_specs=(vmem,) * count,
        scratch_shapes=[
            pltpu.SemaphoreType.DMA((count * (n - 1),)),
            pltpu.SemaphoreType.DMA((count * (n - 1),)),
            pltpu.SemaphoreType.DMA((count,)),
        ],
        compiler_params=pltpu.CompilerParams(collective_id=collective_id, has_side_effects=True),
        cost_estimate=cost(1e9, 1e8),
        name=f"exchange_{collective_id}",
    )(*arrays)


def cost(flops, nbytes):
    return pl.CostEstimate(flops=int(flops), bytes_accessed=int(nbytes), transcendentals=0)


def sum_all(part):
    n_d, n_t = lax.axis_size("dp"), lax.axis_size("tensor")
    _, rank, tokens = part.shape
    q = rank // n_t
    vmem = pl.BlockSpec(memory_space=pltpu.VMEM)
    copies = 2 * (n_d + n_t - 2)
    return pl.pallas_call(
        functools.partial(sum_kernel, n_d, n_t),
        out_shape=jax.ShapeDtypeStruct((n_d, n_t, q, tokens), part.dtype),
        in_specs=[vmem],
        out_specs=vmem,
        scratch_shapes=[
            pltpu.VMEM((n_t - 1, n_d, q, tokens), part.dtype),
            pltpu.VMEM((n_d, q, tokens), part.dtype),
            pltpu.VMEM((n_d - 1, q, tokens), part.dtype),
            pltpu.VMEM((q, tokens), part.dtype),
            pltpu.VMEM((n_d, q, tokens), part.dtype),
            pltpu.SemaphoreType.DMA((copies,)),
            pltpu.SemaphoreType.DMA((copies,)),
        ],
        compiler_params=pltpu.CompilerParams(collective_id=0, has_side_effects=True),
        cost_estimate=cost(1e9, 4e7),
        name="sum_all",
    )(part.reshape(n_d, n_t, q, tokens)).reshape(n_d, rank, tokens)


def project_down(slots, x, w, rank, tokens):
    total_tokens, width = x.shape
    rows = w.shape[0]
    blocks = total_tokens // tokens
    return pl.pallas_call(
        functools.partial(down_kernel, rank),
        out_shape=jax.ShapeDtypeStruct((blocks, rank, tokens), jnp.bfloat16),
        grid=(blocks,),
        in_specs=[
            pl.BlockSpec((1, tokens), lambda i: (0, i)),
            pl.BlockSpec((tokens, width), lambda i: (i, 0)),
            pl.BlockSpec((rows, width), lambda i: (0, 0)),
        ],
        out_specs=pl.BlockSpec((1, rank, tokens), lambda i: (i, 0, 0)),
        cost_estimate=cost(2 * total_tokens * rows * width, 2 * (total_tokens + rows) * width),
        name="down",
    )(slots, x, w)


def project_up(slots, dy, w, rank):
    blocks, dy_rows, tokens = dy.shape
    width, rows = w.shape
    return pl.pallas_call(
        functools.partial(up_kernel, rank),
        out_shape=jax.ShapeDtypeStruct((blocks, rank, tokens), jnp.bfloat16),
        grid=(blocks,),
        in_specs=[
            pl.BlockSpec((1, tokens), lambda i: (0, i)),
            pl.BlockSpec((1, dy_rows, tokens), lambda i: (i, 0, 0)),
            pl.BlockSpec((width, rows), lambda i: (0, 0)),
        ],
        out_specs=pl.BlockSpec((1, rank, tokens), lambda i: (i, 0, 0)),
        cost_estimate=cost(2 * blocks * tokens * rows * width, 4 * (blocks * tokens + rows) * width),
        name="up_back",
    )(slots, dy, w)


def back(slots, up_all, x, w, tokens):
    total_tokens, width = x.shape
    rows = w.shape[0]
    rank = up_all.shape[1]
    blocks = total_tokens // tokens
    return pl.pallas_call(
        back_kernel,
        out_shape=(
            jax.ShapeDtypeStruct((total_tokens, width), jnp.bfloat16),
            jax.ShapeDtypeStruct((rows, width), jnp.bfloat16),
        ),
        grid=(blocks,),
        in_specs=[
            pl.BlockSpec((1, tokens), lambda i: (0, i)),
            pl.BlockSpec((1, rank, tokens), lambda i: (i, 0, 0)),
            pl.BlockSpec((tokens, width), lambda i: (i, 0)),
            pl.BlockSpec((rows, width), lambda i: (0, 0)),
        ],
        out_specs=(
            pl.BlockSpec((tokens, width), lambda i: (i, 0)),
            pl.BlockSpec((rows, width), lambda i: (0, 0)),
        ),
        scratch_shapes=[pltpu.VMEM((rows, width), jnp.float32)],
        cost_estimate=cost(4 * total_tokens * rows * width, 4 * (total_tokens + rows) * width),
        name="back",
    )(slots, up_all, x, w)


def up_grad(slots, down_all, dy, w):
    blocks, dy_rows, tokens = dy.shape
    width, rows = w.shape
    rank = down_all.shape[1]
    return pl.pallas_call(
        up_grad_kernel,
        out_shape=(
            jax.ShapeDtypeStruct((blocks, width, tokens), jnp.bfloat16),
            jax.ShapeDtypeStruct((width, rows), jnp.bfloat16),
        ),
        grid=(blocks,),
        in_specs=[
            pl.BlockSpec((1, tokens), lambda i: (0, i)),
            pl.BlockSpec((1, rank, tokens), lambda i: (i, 0, 0)),
            pl.BlockSpec((1, dy_rows, tokens), lambda i: (i, 0, 0)),
            pl.BlockSpec((width, rows), lambda i: (0, 0)),
        ],
        out_specs=(
            pl.BlockSpec((1, width, tokens), lambda i: (i, 0, 0)),
            pl.BlockSpec((width, rows), lambda i: (0, 0)),
        ),
        scratch_shapes=[pltpu.VMEM((width, rows), jnp.float32)],
        cost_estimate=cost(4 * blocks * tokens * rows * width, 4 * (blocks * tokens + rows) * width),
        name="up_grad",
    )(slots, down_all, dy, w)


def body(
    features,
    key_value_weight,
    adapter_down_weight,
    adapter_up_weight,
    token_adapter_index,
    adapter_position,
    output_gradient,
):
    tokens, width_local = features.shape
    output_local = output_gradient.shape[1]
    local_count, rank, _ = adapter_down_weight.shape
    all_count = adapter_position.shape[0]
    down_matrix = adapter_down_weight.reshape(local_count * rank, width_local)
    up_matrix = adapter_up_weight.reshape(local_count * rank, output_local)

    groups = lax.axis_size("dp")
    part_width = output_local // groups

    def exchange(array, split, concat):
        return lax.all_to_all(array, "dp", split_axis=split, concat_axis=concat, tiled=True)

    ids = jnp.arange(all_count, dtype=jnp.int32)
    matches = token_adapter_index[:, None] == ids[None, :]
    slot_tok = jnp.sum(jnp.where(matches, adapter_position[None, :], 0), axis=1)
    digits = jnp.stack([slot_tok // 64, slot_tok % 64]).astype(jnp.bfloat16)
    pad_rows = (-part_width - 2) % 16
    tail = jnp.concatenate([digits, jnp.zeros((pad_rows, tokens), jnp.bfloat16)], axis=0)
    dy_send = jnp.concatenate(
        [
            output_gradient.T.reshape(groups, part_width, tokens),
            jnp.broadcast_to(tail[None], (groups, 2 + pad_rows, tokens)),
        ],
        axis=1,
    )
    own_rows = local_count * rank
    all_rows = own_rows * groups
    in_width = width_local // groups
    direct = in_width % 128 == 0 and own_rows % 128 == 0 and part_width % 16 == 0
    if direct:
        dy_cols, up_cols, down_cols = exchange_all(
            (dy_send, up_matrix.T.reshape(groups, part_width, own_rows), down_matrix),
            (dy_send.shape, (part_width, all_rows), (groups, own_rows, in_width)),
            (("lead", "lead"), ("lead", "col"), ("col", "lead")),
            1,
        )
        down_cols = down_cols.reshape(all_rows, in_width)
    else:
        dy_cols = exchange(dy_send, 0, 0)
        up_cols = exchange(up_matrix.T, 0, 1)
        down_cols = exchange(down_matrix, 1, 0)
    got = dy_cols[:, part_width : part_width + 2].astype(jnp.int32)
    slots_all = (got[:, 0] * 64 + got[:, 1]).reshape(1, groups * tokens)

    feature_cols = exchange(features, 1, 0)

    up_all = sum_all(project_up(slots_all, dy_cols, up_cols, rank))
    in_cols, down_grad_cols = back(slots_all, up_all, feature_cols, down_cols, tokens)
    in_cols, slots_late = lax.optimization_barrier((in_cols, slots_all))
    lora_in = exchange(in_cols, 0, 1)

    down_all = sum_all(project_down(slots_late, feature_cols, down_cols, rank, tokens))
    out_cols, up_grad_cols = up_grad(slots_all, down_all, dy_cols, up_cols)
    if direct:
        lora_out, up_gradient, down_gradient = exchange_all(
            (out_cols, up_grad_cols, down_grad_cols.reshape(groups, own_rows, in_width)),
            (out_cols.shape, (groups, part_width, own_rows), (own_rows, width_local)),
            (("lead", "lead"), ("col", "lead"), ("lead", "col")),
            2,
        )
        up_gradient = up_gradient.reshape(output_local, own_rows)
    else:
        lora_out = exchange(out_cols, 0, 0)
        up_gradient = exchange(up_grad_cols, 1, 0)
        down_gradient = exchange(down_grad_cols, 0, 1)
    lora_out = lora_out.reshape(output_local, tokens)

    gradient_frozen = dot_dims(
        lax.all_gather(output_gradient, "tensor", axis=1, tiled=True), key_value_weight, 1, 1
    )
    key_value_frozen = lax.psum_scatter(
        dot_dims(key_value_weight, features, 0, 1), "tensor", scatter_dimension=0, tiled=True
    )
    key_value_output = (key_value_frozen + lora_out.astype(jnp.float32)).astype(jnp.bfloat16).T
    feature_gradient = (gradient_frozen + lora_in.astype(jnp.float32)).astype(jnp.bfloat16)
    return (
        key_value_output,
        feature_gradient,
        down_gradient.astype(jnp.float32).reshape(local_count, rank, width_local),
        up_gradient.astype(jnp.float32).T.reshape(local_count, rank, output_local),
    )


def solution(mesh):
    placed = (
        P("dp", "tensor"),
        P("tensor", None),
        P("dp", None, "tensor"),
        P("dp", None, "tensor"),
        P("dp"),
        P(),
        P("dp", "tensor"),
    )
    return jax.shard_map(
        body,
        mesh=mesh,
        in_specs=placed,
        out_specs=(
            P("dp", "tensor"),
            P("dp", "tensor"),
            P("dp", None, "tensor"),
            P("dp", None, "tensor"),
        ),
        check_vma=False,
    )
```

```python
import functools

import jax
import jax.numpy as jnp
from jax import lax
from jax.experimental import pallas as pl
from jax.experimental.pallas import tpu as pltpu
from jax.sharding import PartitionSpec as P

adapter_scale = 2.0


def dot_dims(left, right, left_dim, right_dim):
    return lax.dot_general(
        left, right, (((left_dim,), (right_dim,)), ((), ())), preferred_element_type=jnp.float32
    )


def slot_mask(slot_row, rank, rows):
    tokens = slot_row.shape[1]
    row_slot = lax.broadcasted_iota(jnp.int32, (rows, tokens), 0) // rank
    return row_slot == slot_row


def fold_slots(full, slot_row, rank):
    rows, tokens = full.shape
    kept = jnp.where(slot_mask(slot_row, rank, rows), full, 0.0)
    return jnp.sum(kept.reshape(rows // rank, rank, tokens), axis=0)


def down_kernel(rank, slot_ref, x_ref, w_ref, o_ref):
    full = dot_dims(w_ref[...], x_ref[...], 1, 1)
    o_ref[0] = fold_slots(full, slot_ref[...], rank).astype(o_ref.dtype)


def up_kernel(rank, slot_ref, dy_ref, w_ref, o_ref):
    full = dot_dims(w_ref[...], dy_ref[0, : w_ref.shape[0]], 0, 0)
    o_ref[0] = (adapter_scale * fold_slots(full, slot_ref[...], rank)).astype(o_ref.dtype)


def widen(values, slot_row, rows):
    rank = values.shape[0]
    tiled = jnp.tile(values.astype(jnp.float32), (rows // rank, 1))
    return jnp.where(slot_mask(slot_row, rank, rows), tiled, 0.0).astype(jnp.bfloat16)


def back_kernel(slot_ref, up_ref, x_ref, w_ref, rows_ref, grad_ref, total):
    step = pl.program_id(0)
    wide = widen(up_ref[0], slot_ref[...], w_ref.shape[0])
    rows_ref[...] = dot_dims(wide, w_ref[...], 0, 0).astype(rows_ref.dtype)
    part = jnp.dot(wide, x_ref[...], preferred_element_type=jnp.float32)

    @pl.when(step == 0)
    def _():
        total[...] = part

    @pl.when(step > 0)
    def _():
        total[...] += part

    @pl.when(step == pl.num_programs(0) - 1)
    def _():
        grad_ref[...] = total[...].astype(grad_ref.dtype)


def up_grad_kernel(slot_ref, down_ref, dy_ref, w_ref, rows_ref, grad_ref, total):
    step = pl.program_id(0)
    width, rows = w_ref.shape
    wide = widen(down_ref[0], slot_ref[...], rows)
    out = jnp.dot(w_ref[...], wide, preferred_element_type=jnp.float32)
    rows_ref[0] = (adapter_scale * out).astype(rows_ref.dtype)
    part = dot_dims(dy_ref[0, :width], wide, 1, 1)

    @pl.when(step == 0)
    def _():
        total[...] = part

    @pl.when(step > 0)
    def _():
        total[...] += part

    @pl.when(step == pl.num_programs(0) - 1)
    def _():
        grad_ref[...] = (adapter_scale * total[...]).astype(grad_ref.dtype)


def sum_kernel(n_d, n_t, part_ref, out_ref, from_t, own_t, from_d, own_d, all_d, send, recv):
    me_d, me_t = lax.axis_index("dp"), lax.axis_index("tensor")
    peers_d = [lax.rem(me_d + k, n_d) for k in range(n_d)]
    peers_t = [lax.rem(me_t + k, n_t) for k in range(n_t)]

    barrier = pltpu.get_barrier_semaphore()
    for peer in peers_t[1:]:
        pl.semaphore_signal(
            barrier, inc=1, device_id=(me_d, peer), device_id_type=pl.DeviceIdType.MESH
        )
    for peer in peers_d[1:]:
        pl.semaphore_signal(
            barrier, inc=1, device_id=(peer, me_t), device_id_type=pl.DeviceIdType.MESH
        )
    pl.semaphore_wait(barrier, n_d + n_t - 2)

    base = 0

    def copy(src, dst, device, index):
        made = pltpu.make_async_remote_copy(
            src_ref=src,
            dst_ref=dst,
            send_sem=send.at[index],
            recv_sem=recv.at[index],
            device_id=device,
            device_id_type=pl.DeviceIdType.MESH,
        )
        made.start()
        return made

    made = [
        copy(part_ref.at[:, peers_t[k]], from_t.at[k - 1], (me_d, peers_t[k]), base + k - 1)
        for k in range(1, n_t)
    ]
    base += n_t - 1
    for one in made:
        one.wait()
    total = part_ref[:, me_t].astype(jnp.float32)
    for k in range(n_t - 1):
        total = total + from_t[k].astype(jnp.float32)
    own_t[...] = total.astype(own_t.dtype)

    made = [
        copy(own_t.at[peers_d[k]], from_d.at[k - 1], (peers_d[k], me_t), base + k - 1)
        for k in range(1, n_d)
    ]
    base += n_d - 1
    for one in made:
        one.wait()
    total = own_t[me_d].astype(jnp.float32)
    for k in range(n_d - 1):
        total = total + from_d[k].astype(jnp.float32)
    own_d[...] = total.astype(own_d.dtype)

    made = [
        copy(own_d, all_d.at[me_d], (peers_d[k], me_t), base + k - 1) for k in range(1, n_d)
    ]
    base += n_d - 1
    all_d[me_d] = own_d[...]
    for one in made:
        one.wait()

    made = [
        copy(all_d, out_ref.at[:, me_t], (me_d, peers_t[k]), base + k - 1)
        for k in range(1, n_t)
    ]
    out_ref[:, me_t] = all_d[...]
    for one in made:
        one.wait()


def block_view(ref, form, index, n):
    if form == "lead":
        return ref.at[index]
    width = ref.shape[1] // n
    return ref.at[:, pl.ds(pl.multiple_of(index * width, width), width)]


def exchange_kernel(n, forms, *refs):
    count = len(forms)
    sources, targets = refs[:count], refs[count : 2 * count]
    send, recv, own = refs[2 * count :]
    me_d, me_t = lax.axis_index("dp"), lax.axis_index("tensor")
    peers = [lax.rem(me_d + k, n) for k in range(n)]
    barrier = pltpu.get_barrier_semaphore()
    for peer in peers[1:]:
        pl.semaphore_signal(
            barrier, inc=1, device_id=(peer, me_t), device_id_type=pl.DeviceIdType.MESH
        )
    pl.semaphore_wait(barrier, n - 1)
    made = []
    for at, (source_form, target_form) in enumerate(forms):
        for k in range(1, n):
            made.append(
                pltpu.make_async_remote_copy(
                    src_ref=block_view(sources[at], source_form, peers[k], n),
                    dst_ref=block_view(targets[at], target_form, me_d, n),
                    send_sem=send.at[at * (n - 1) + k - 1],
                    recv_sem=recv.at[at * (n - 1) + k - 1],
                    device_id=(peers[k], me_t),
                    device_id_type=pl.DeviceIdType.MESH,
                )
            )
            made[-1].start()
    for at, (source_form, target_form) in enumerate(forms):
        made.append(
            pltpu.make_async_copy(
                block_view(sources[at], source_form, me_d, n),
                block_view(targets[at], target_form, me_d, n),
                own.at[at],
            )
        )
        made[-1].start()
    for one in made:
        one.wait()


def exchange_all(arrays, shapes, forms, collective_id):
    n = lax.axis_size("dp")
    vmem = pl.BlockSpec(memory_space=pltpu.VMEM)
    count = len(arrays)
    return pl.pallas_call(
        functools.partial(exchange_kernel, n, forms),
        out_shape=tuple(jax.ShapeDtypeStruct(shape, jnp.bfloat16) for shape in shapes),
        in_specs=[vmem] * count,
        out_specs=(vmem,) * count,
        scratch_shapes=[
            pltpu.SemaphoreType.DMA((count * (n - 1),)),
            pltpu.SemaphoreType.DMA((count * (n - 1),)),
            pltpu.SemaphoreType.DMA((count,)),
        ],
        compiler_params=pltpu.CompilerParams(collective_id=collective_id, has_side_effects=True),
        cost_estimate=cost(1e9, 1e8),
        name=f"exchange_{collective_id}",
    )(*arrays)


def cost(flops, nbytes):
    return pl.CostEstimate(flops=int(flops), bytes_accessed=int(nbytes), transcendentals=0)


def sum_all(part):
    n_d, n_t = lax.axis_size("dp"), lax.axis_size("tensor")
    _, rank, tokens = part.shape
    q = rank // n_t
    vmem = pl.BlockSpec(memory_space=pltpu.VMEM)
    copies = 2 * (n_d + n_t - 2)
    return pl.pallas_call(
        functools.partial(sum_kernel, n_d, n_t),
        out_shape=jax.ShapeDtypeStruct((n_d, n_t, q, tokens), part.dtype),
        in_specs=[vmem],
        out_specs=vmem,
        scratch_shapes=[
            pltpu.VMEM((n_t - 1, n_d, q, tokens), part.dtype),
            pltpu.VMEM((n_d, q, tokens), part.dtype),
            pltpu.VMEM((n_d - 1, q, tokens), part.dtype),
            pltpu.VMEM((q, tokens), part.dtype),
            pltpu.VMEM((n_d, q, tokens), part.dtype),
            pltpu.SemaphoreType.DMA((copies,)),
            pltpu.SemaphoreType.DMA((copies,)),
        ],
        compiler_params=pltpu.CompilerParams(collective_id=0, has_side_effects=True),
        cost_estimate=cost(1e9, 4e7),
        name="sum_all",
    )(part.reshape(n_d, n_t, q, tokens)).reshape(n_d, rank, tokens)


def project_down(slots, x, w, rank, tokens):
    total_tokens, width = x.shape
    rows = w.shape[0]
    blocks = total_tokens // tokens
    return pl.pallas_call(
        functools.partial(down_kernel, rank),
        out_shape=jax.ShapeDtypeStruct((blocks, rank, tokens), jnp.bfloat16),
        grid=(blocks,),
        in_specs=[
            pl.BlockSpec((1, tokens), lambda i: (0, i)),
            pl.BlockSpec((tokens, width), lambda i: (i, 0)),
            pl.BlockSpec((rows, width), lambda i: (0, 0)),
        ],
        out_specs=pl.BlockSpec((1, rank, tokens), lambda i: (i, 0, 0)),
        cost_estimate=cost(2 * total_tokens * rows * width, 2 * (total_tokens + rows) * width),
        name="down",
    )(slots, x, w)


def project_up(slots, dy, w, rank):
    blocks, dy_rows, tokens = dy.shape
    width, rows = w.shape
    return pl.pallas_call(
        functools.partial(up_kernel, rank),
        out_shape=jax.ShapeDtypeStruct((blocks, rank, tokens), jnp.bfloat16),
        grid=(blocks,),
        in_specs=[
            pl.BlockSpec((1, tokens), lambda i: (0, i)),
            pl.BlockSpec((1, dy_rows, tokens), lambda i: (i, 0, 0)),
            pl.BlockSpec((width, rows), lambda i: (0, 0)),
        ],
        out_specs=pl.BlockSpec((1, rank, tokens), lambda i: (i, 0, 0)),
        cost_estimate=cost(2 * blocks * tokens * rows * width, 4 * (blocks * tokens + rows) * width),
        name="up_back",
    )(slots, dy, w)


def back(slots, up_all, x, w, tokens):
    total_tokens, width = x.shape
    rows = w.shape[0]
    rank = up_all.shape[1]
    blocks = total_tokens // tokens
    return pl.pallas_call(
        back_kernel,
        out_shape=(
            jax.ShapeDtypeStruct((total_tokens, width), jnp.bfloat16),
            jax.ShapeDtypeStruct((rows, width), jnp.bfloat16),
        ),
        grid=(blocks,),
        in_specs=[
            pl.BlockSpec((1, tokens), lambda i: (0, i)),
            pl.BlockSpec((1, rank, tokens), lambda i: (i, 0, 0)),
            pl.BlockSpec((tokens, width), lambda i: (i, 0)),
            pl.BlockSpec((rows, width), lambda i: (0, 0)),
        ],
        out_specs=(
            pl.BlockSpec((tokens, width), lambda i: (i, 0)),
            pl.BlockSpec((rows, width), lambda i: (0, 0)),
        ),
        scratch_shapes=[pltpu.VMEM((rows, width), jnp.float32)],
        cost_estimate=cost(4 * total_tokens * rows * width, 4 * (total_tokens + rows) * width),
        name="back",
    )(slots, up_all, x, w)


def up_grad(slots, down_all, dy, w):
    blocks, dy_rows, tokens = dy.shape
    width, rows = w.shape
    rank = down_all.shape[1]
    return pl.pallas_call(
        up_grad_kernel,
        out_shape=(
            jax.ShapeDtypeStruct((blocks, width, tokens), jnp.bfloat16),
            jax.ShapeDtypeStruct((width, rows), jnp.bfloat16),
        ),
        grid=(blocks,),
        in_specs=[
            pl.BlockSpec((1, tokens), lambda i: (0, i)),
            pl.BlockSpec((1, rank, tokens), lambda i: (i, 0, 0)),
            pl.BlockSpec((1, dy_rows, tokens), lambda i: (i, 0, 0)),
            pl.BlockSpec((width, rows), lambda i: (0, 0)),
        ],
        out_specs=(
            pl.BlockSpec((1, width, tokens), lambda i: (i, 0, 0)),
            pl.BlockSpec((width, rows), lambda i: (0, 0)),
        ),
        scratch_shapes=[pltpu.VMEM((width, rows), jnp.float32)],
        cost_estimate=cost(4 * blocks * tokens * rows * width, 4 * (blocks * tokens + rows) * width),
        name="up_grad",
    )(slots, down_all, dy, w)


def body(
    features,
    key_value_weight,
    adapter_down_weight,
    adapter_up_weight,
    token_adapter_index,
    adapter_position,
    output_gradient,
):
    tokens, width_local = features.shape
    output_local = output_gradient.shape[1]
    local_count, rank, _ = adapter_down_weight.shape
    all_count = adapter_position.shape[0]
    down_matrix = adapter_down_weight.reshape(local_count * rank, width_local)
    up_matrix = adapter_up_weight.reshape(local_count * rank, output_local)

    groups = lax.axis_size("dp")
    part_width = output_local // groups

    def exchange(array, split, concat):
        return lax.all_to_all(array, "dp", split_axis=split, concat_axis=concat, tiled=True)

    ids = jnp.arange(all_count, dtype=jnp.int32)
    matches = token_adapter_index[:, None] == ids[None, :]
    slot_tok = jnp.sum(jnp.where(matches, adapter_position[None, :], 0), axis=1)
    digits = jnp.stack([slot_tok // 64, slot_tok % 64]).astype(jnp.bfloat16)
    pad_rows = (-part_width - 2) % 16
    tail = jnp.concatenate([digits, jnp.zeros((pad_rows, tokens), jnp.bfloat16)], axis=0)
    dy_send = jnp.concatenate(
        [
            output_gradient.T.reshape(groups, part_width, tokens),
            jnp.broadcast_to(tail[None], (groups, 2 + pad_rows, tokens)),
        ],
        axis=1,
    )
    own_rows = local_count * rank
    all_rows = own_rows * groups
    in_width = width_local // groups
    direct = in_width % 128 == 0 and own_rows % 128 == 0 and part_width % 16 == 0
    if direct:
        dy_cols, up_cols, down_cols = exchange_all(
            (dy_send, up_matrix.T.reshape(groups, part_width, own_rows), down_matrix),
            (dy_send.shape, (part_width, all_rows), (groups, own_rows, in_width)),
            (("lead", "lead"), ("lead", "col"), ("col", "lead")),
            1,
        )
        down_cols = down_cols.reshape(all_rows, in_width)
    else:
        dy_cols = exchange(dy_send, 0, 0)
        up_cols = exchange(up_matrix.T, 0, 1)
        down_cols = exchange(down_matrix, 1, 0)
    got = dy_cols[:, part_width : part_width + 2].astype(jnp.int32)
    slots_all = (got[:, 0] * 64 + got[:, 1]).reshape(1, groups * tokens)

    late, slots_all = lax.optimization_barrier((features, slots_all))
    feature_cols = exchange(late, 1, 0)

    up_all = sum_all(project_up(slots_all, dy_cols, up_cols, rank))
    in_cols, down_grad_cols = back(slots_all, up_all, feature_cols, down_cols, tokens)
    in_cols, slots_late = lax.optimization_barrier((in_cols, slots_all))
    lora_in = exchange(in_cols, 0, 1)

    down_all = sum_all(project_down(slots_late, feature_cols, down_cols, rank, tokens))
    out_cols, up_grad_cols = up_grad(slots_all, down_all, dy_cols, up_cols)
    if direct:
        lora_out, up_gradient, down_gradient = exchange_all(
            (out_cols, up_grad_cols, down_grad_cols.reshape(groups, own_rows, in_width)),
            (out_cols.shape, (groups, part_width, own_rows), (own_rows, width_local)),
            (("lead", "lead"), ("col", "lead"), ("lead", "col")),
            2,
        )
        up_gradient = up_gradient.reshape(output_local, own_rows)
    else:
        lora_out = exchange(out_cols, 0, 0)
        up_gradient = exchange(up_grad_cols, 1, 0)
        down_gradient = exchange(down_grad_cols, 0, 1)
    lora_out = lora_out.reshape(output_local, tokens)

    gradient_frozen = dot_dims(
        lax.all_gather(output_gradient, "tensor", axis=1, tiled=True), key_value_weight, 1, 1
    )
    key_value_frozen = lax.psum_scatter(
        dot_dims(key_value_weight, features, 0, 1), "tensor", scatter_dimension=0, tiled=True
    )
    key_value_output = (key_value_frozen + lora_out.astype(jnp.float32)).astype(jnp.bfloat16).T
    feature_gradient = (gradient_frozen + lora_in.astype(jnp.float32)).astype(jnp.bfloat16)
    return (
        key_value_output,
        feature_gradient,
        down_gradient.astype(jnp.float32).reshape(local_count, rank, width_local),
        up_gradient.astype(jnp.float32).T.reshape(local_count, rank, output_local),
    )


def solution(mesh):
    placed = (
        P("dp", "tensor"),
        P("tensor", None),
        P("dp", None, "tensor"),
        P("dp", None, "tensor"),
        P("dp"),
        P(),
        P("dp", "tensor"),
    )
    return jax.shard_map(
        body,
        mesh=mesh,
        in_specs=placed,
        out_specs=(
            P("dp", "tensor"),
            P("dp", "tensor"),
            P("dp", None, "tensor"),
            P("dp", None, "tensor"),
        ),
        check_vma=False,
    )
```
